32 devices in a mesh: grp: 2 (over y), blk: 8 (over z, x), cross: 2 (over core).
Axes of the slice: x: 2, y: 2, z: 4, core: 2. Of those that a mesh axis runs over, the one named last changes fastest.
Arguments:
- orbitals: bfloat16 [32, 40, 1600], P(('grp', 'blk', 'cross')), parts along dimension 0, may hold values from -6 to 6
- response: bfloat16 [32, 40, 1600], P(('grp', 'blk', 'cross')), parts along dimension 0, may hold values from -6 to 6
- pair_mask: int32 [32, 4], P(('grp', 'blk', 'cross')), parts along dimension 0, may hold values 0 or 1
Outputs:
- tangent_exchange: bfloat16 [32, 40, 1600], P(('grp', 'blk', 'cross')), parts along dimension 0
The draws below stay inside these ranges and needn't reach their ends.
There are 2 independent parts, one for each index of `grp`. The reference program is written for one: setup_inputs(seed, part) draws one part's arguments, and reference() takes and returns one part's arrays. A program takes and returns all parts, laid end to end along the dimension named above; each array names one. Nothing has to cross between parts.
All inputs are finite; a program needn't handle non-finite values. No bound on the sum of `pair_mask` on one device may be relied on, other than what follows from the above.
Results may differ from the reference program's by a relative error of at most 0.017.
Values may be sent and summed in bfloat16 or wider, within the bound.
A program may use at most 64 MiB of HBM per device.

```python
import jax
import jax.numpy as jnp
from jax import lax

NG = 40
ORBS = 16


def with_ends(result, stream_key, least, high):
    place = [jax.random.randint(jax.random.fold_in(stream_key, axis), (), 0, length) for axis, length in enumerate(result.shape)]
    longest = result.shape.index(max(result.shape))
    neighbour = place[:longest] + [(place[longest] + 1) % result.shape[longest]] + place[longest + 1:]
    return result.at[tuple(place)].set(least).at[tuple(neighbour)].set(high)


def block_levels(own_key, dims, pieces, low, top_value):
    gain, own = 1.0, jax.random.fold_in(own_key, 6)
    for axis_at, parts in pieces:
        draws = jnp.exp(jax.random.uniform(jax.random.fold_in(own, axis_at), (parts,), jnp.float32, low / len(pieces), top_value / len(pieces)))
        gain = gain * jnp.repeat(draws, dims[axis_at] // parts).reshape([-1 if axis == axis_at else 1 for axis in range(len(dims))])
    return gain


def centred(stream_key, dims, scale, bound, split=(), held_as=jnp.bfloat16):
    drawn = scale * jax.random.normal(stream_key, dims, jnp.float32)
    if split:
        drawn = drawn * block_levels(stream_key, dims, split, -0.22, 0.18)
    return jnp.clip(drawn, -bound, bound).astype(held_as)


def setup_inputs(seed: int = 0, part: int = 0) -> dict:
    key_of = jax.random.split(jax.random.key(seed), 4)
    own_keys = jax.random.split(jax.random.fold_in(key_of[3], part), 4)
    return {
        "orbitals": centred(own_keys[0], (ORBS, NG, NG * NG), 1.0, 6.0, ((0, 16),)),
        "response": centred(own_keys[1], (ORBS, NG, NG * NG), 1.0, 6.0, ((0, 16),)),
        "pair_mask": with_ends((jax.random.randint(own_keys[2], (ORBS, 4), 0, 4) < 3).astype(jnp.int32), jax.random.fold_in(own_keys[2], 1), 0, 1),
    }


mixing = 0.25

def dft_tables(length):
    positions = jnp.arange(length, dtype=jnp.int32)
    phases = positions[:, None] * positions[None, :] % length
    angles = phases.astype(jnp.float32) * (2.0 * jnp.pi / length)
    scaling = 1.0 / jnp.sqrt(jnp.float32(length))
    cosine = (jnp.cos(angles) * scaling).astype(jnp.bfloat16)
    sines = (jnp.sin(angles) * scaling).astype(jnp.bfloat16)
    forward = jnp.concatenate([jnp.concatenate([cosine, sines], 1), jnp.concatenate([-sines, cosine], 1)], 0)
    inverse = jnp.concatenate([jnp.concatenate([cosine, -sines], 1), jnp.concatenate([sines, cosine], 1)], 0)
    return (forward, inverse)

def coulomb(length):
    positions = jnp.arange(length, dtype=jnp.int32)
    frequency = jnp.where(positions <= length // 2, positions, positions - length).astype(jnp.float32)
    squares = frequency * frequency
    norm_squared = squares[:, None, None] + squares[None, :, None] + squares[None, None, :]
    values = 1.0 / (0.0625 + 25.0 * norm_squared / (length * length))
    values = jnp.where(norm_squared > 0.5, values, jnp.float32(0.0))
    return values.reshape(length, length * length)

def apply_section(matrix, stacked):
    length = stacked.shape[0] // 2
    product = jnp.dot(matrix, stacked, preferred_element_type=jnp.float32).astype(jnp.bfloat16)
    volume = product.reshape(2, length, length, length)
    return jnp.transpose(volume, (0, 2, 3, 1)).reshape(2 * length, length * length)

def potentials(own_orbital, own_response, far_orbital, far_response, forward, inverse, kernel):
    length = own_orbital.shape[0]
    own_f = own_orbital.astype(jnp.float32)
    far_f = far_orbital.astype(jnp.float32)
    ground = (own_f * far_f).astype(jnp.bfloat16)
    tangent = (own_response.astype(jnp.float32) * far_f + own_f * far_response.astype(jnp.float32)).astype(jnp.bfloat16)
    spectrum = jnp.concatenate([ground, tangent], 0)
    for repeat in range(3):
        spectrum = apply_section(forward, spectrum)
    filtered = (spectrum.reshape(2, length, -1).astype(jnp.float32) * kernel[None]).astype(jnp.bfloat16)
    filtered = filtered.reshape(2 * length, -1)
    for repeat in range(3):
        filtered = apply_section(inverse, filtered)
    return (filtered[:length], filtered[length:])

def contribution(partner, partner_response, ground, tangent):
    return (partner_response.astype(jnp.float32) * ground.astype(jnp.float32) + partner.astype(jnp.float32) * tangent.astype(jnp.float32)).astype(jnp.bfloat16)

def reference(orbitals, response, pair_mask):
    forward, inverse = dft_tables(NG)
    kernel = coulomb(NG)

    def both_terms(items):
        own_orbital, own_response, far_orbital, far_response = items
        ground, tangent = potentials(own_orbital, own_response, far_orbital, far_response, forward, inverse, kernel)
        return (contribution(far_orbital, far_response, ground, tangent), contribution(own_orbital, own_response, ground, tangent))
    self_term = lax.map(lambda items: both_terms((items[0], items[1], items[0], items[1]))[0], (orbitals, response))
    later_orbital = jnp.roll(orbitals, -2, 0)
    later_response = jnp.roll(response, -2, 0)
    later_term, handed = lax.map(both_terms, (orbitals, response, later_orbital, later_response))
    prior_term = jnp.roll(handed, 2, 0)
    even_term, odd_term = lax.map(both_terms, (orbitals[0::2], response[0::2], orbitals[1::2], response[1::2]))
    mate_term = jnp.stack([even_term, odd_term], 1).reshape(orbitals.shape)
    weights = pair_mask.astype(jnp.float32)
    total = weights[:, 0, None, None] * self_term.astype(jnp.float32) + weights[:, 1, None, None] * mate_term.astype(jnp.float32) + weights[:, 2, None, None] * prior_term.astype(jnp.float32) + weights[:, 3, None, None] * later_term.astype(jnp.float32)
    return (-mixing * total).astype(jnp.bfloat16)
```

```python
import functools

import jax
import jax.numpy as jnp
import numpy as np
from jax import lax
from jax.experimental import pallas as pl
from jax.experimental.pallas import tpu as pltpu
from jax.sharding import PartitionSpec as P

mixing = 0.25
MESH = pl.DeviceIdType.MESH
f32, bf16 = jnp.float32, jnp.bfloat16


def cas_table(length):
    positions = np.arange(length)
    angles = (positions[:, None] * positions[None, :] % length) * (2.0 * np.pi / length)
    return (np.cos(angles) + np.sin(angles)) / np.sqrt(length)


def coulomb(length):
    positions = np.arange(length)
    frequency = np.where(positions <= length // 2, positions, positions - length).astype(float)
    squares = frequency * frequency
    norm_squared = squares[:, None, None] + squares[None, :, None] + squares[None, None, :]
    values = 1.0 / (0.0625 + 25.0 * norm_squared / (length * length))
    values = np.where(norm_squared > 0.5, values, 0.0)
    return values.reshape(length, length * length)


def pieces(total, step=256):
    return [(at, min(step, total - at)) for at in range(0, total, step)]


def kernel(
    blks,
    orb_ref, resp_ref, mask_ref, zt_ref, yt_ref, left_ref, coul_ref,
    out_ref,
    planes, mid, mate, prior, handed, later, total,
    send_sem, recv_sem,
):
    grp, blk, cross = lax.axis_index("grp"), lax.axis_index("blk"), lax.axis_index("cross")
    length, area = orb_ref.shape[1:]
    to_mate = (grp, blk, 1 - cross)
    to_next = (grp, lax.rem(blk + 1, blks), cross)
    to_prev = (grp, lax.rem(blk + blks - 1, blks), cross)

    barrier = pltpu.get_barrier_semaphore()
    for device in (to_mate, to_next, to_prev):
        pl.semaphore_signal(barrier, inc=1, device_id=device, device_id_type=MESH)
    pl.semaphore_wait(barrier, 3)

    def remote(src, dst, slot, device):
        return pltpu.make_async_remote_copy(
            src_ref=src, dst_ref=dst, send_sem=send_sem.at[slot], recv_sem=recv_sem.at[slot],
            device_id=device, device_id_type=MESH,
        )

    copies = [
        remote(orb_ref.at[0], prior.at[0], 0, to_next),
        remote(resp_ref.at[0], prior.at[1], 1, to_next),
        remote(orb_ref.at[0], mate.at[0], 2, to_mate),
        remote(resp_ref.at[0], mate.at[1], 3, to_mate),
    ]
    for copy in copies:
        copy.start()

    inner = zt_ref[...]

    def fill(pair, carry):
        at = pl.multiple_of(pair * 2 * length, 2 * length)
        rows = yt_ref[pair]
        both = jnp.concatenate([inner * rows[0:1], inner * rows[1:2]], 0)
        planes[pl.ds(at, 2 * length), :] = both.astype(bf16)
        return carry

    lax.fori_loop(0, length // 2, fill, 0)

    own_orb, own_resp = orb_ref[0].astype(f32), resp_ref[0].astype(f32)

    def densities(far_orb, far_resp):
        orb, resp = orb_ref[0].astype(f32), resp_ref[0].astype(f32)
        return jnp.concatenate([orb * far_orb, resp * far_orb + orb * far_resp], 0).astype(bf16)

    def transform(values, rows):
        for at, width in pieces(area):
            mid[:rows, at:at + width] = jnp.dot(
                values, planes[:, at:at + width], preferred_element_type=f32
            ).astype(bf16)
        for first in range(0, rows, 2 * length):
            for at, width in pieces(area):
                part = mid[first:first + 2 * length, at:at + width]
                spectrum = jnp.dot(left_ref[...], part, preferred_element_type=f32)
                scale = coul_ref[:, at:at + width]
                filtered = (spectrum * jnp.concatenate([scale, scale], 0)).astype(bf16)
                back = jnp.dot(left_ref[...], filtered, preferred_element_type=f32)
                mid[first:first + 2 * length, at:at + width] = back.astype(bf16)

    weight = [mask_ref[0, k].astype(f32) for k in range(4)]

    copies[2].wait()
    copies[3].wait()
    rows = 4 * length
    first = densities(orb_ref[0].astype(f32), resp_ref[0].astype(f32))
    second = densities(mate[0].astype(f32), mate[1].astype(f32))
    transform(jnp.concatenate([first, second], 0), rows)
    for at, width in pieces(area):
        here = slice(at, at + width)
        fields = jnp.dot(mid[:rows], planes[:, here], preferred_element_type=f32)
        v0, d0 = fields[:length], fields[length:2 * length]
        v1, d1 = fields[2 * length:3 * length], fields[3 * length:]
        total[:, here] = weight[0] * (
            resp_ref[0, :, here].astype(f32) * v0 + orb_ref[0, :, here].astype(f32) * d0
        ) + weight[1] * (mate[1, :, here].astype(f32) * v1 + mate[0, :, here].astype(f32) * d1)

    copies[0].wait()
    copies[1].wait()
    rows = 2 * length
    transform(densities(prior[0].astype(f32), prior[1].astype(f32)), rows)
    for at, width in pieces(area):
        here = slice(at, at + width)
        fields = jnp.dot(mid[:rows], planes[:, here], preferred_element_type=f32)
        v, d = fields[:length], fields[length:]
        handed[:, here] = (
            resp_ref[0, :, here].astype(f32) * v + orb_ref[0, :, here].astype(f32) * d
        ).astype(bf16)
        total[:, here] += weight[2] * (
            prior[1, :, here].astype(f32) * v + prior[0, :, here].astype(f32) * d
        )
    back = remote(handed, later, 4, to_prev)
    back.start()
    back.wait()
    out_ref[0] = (-mixing * (total[...] + weight[3] * later[...].astype(f32))).astype(bf16)


def shards(blks, orbitals, response, pair_mask):
    length, area = orbitals.shape[1:]
    table = cas_table(length)
    inner = np.tile(table, (1, length)).astype(np.float32)
    outer = np.repeat(table, length, 1).astype(np.float32).reshape(length // 2, 2, area)
    left = jnp.asarray(np.kron(np.eye(2), table), bf16)
    kernel_values = coulomb(length).astype(np.float32)
    vmem = pl.BlockSpec(memory_space=pltpu.VMEM)
    return pl.pallas_call(
        functools.partial(kernel, blks),
        out_shape=jax.ShapeDtypeStruct(orbitals.shape, orbitals.dtype),
        in_specs=[vmem, vmem, pl.BlockSpec(memory_space=pltpu.SMEM), vmem, vmem, vmem, vmem],
        out_specs=vmem,
        scratch_shapes=[
            pltpu.VMEM((area, area), bf16),
            pltpu.VMEM((4 * length, area), bf16),
            pltpu.VMEM((2, length, area), bf16),
            pltpu.VMEM((2, length, area), bf16),
            pltpu.VMEM((length, area), bf16),
            pltpu.VMEM((length, area), bf16),
            pltpu.VMEM((length, area), f32),
            pltpu.SemaphoreType.DMA((5,)),
            pltpu.SemaphoreType.DMA((5,)),
        ],
        compiler_params=pltpu.CompilerParams(collective_id=0, has_side_effects=True),
    )(orbitals, response, pair_mask, inner, outer, left, kernel_values)


def solution(mesh):
    spec = P(("grp", "blk", "cross"), None, None)
    return jax.shard_map(
        functools.partial(shards, mesh.shape["blk"]),
        mesh=mesh,
        in_specs=(spec, spec, P(("grp", "blk", "cross"), None)),
        out_specs=spec,
        check_vma=False,
    )
```

```python
import functools

import jax
import jax.numpy as jnp
import numpy as np
from jax import lax
from jax.experimental import pallas as pl
from jax.experimental.pallas import tpu as pltpu
from jax.sharding import PartitionSpec as P

mixing = 0.25
MESH = pl.DeviceIdType.MESH
f32, bf16 = jnp.float32, jnp.bfloat16


def cas_table(length):
    positions = np.arange(length)
    angles = (positions[:, None] * positions[None, :] % length) * (2.0 * np.pi / length)
    return (np.cos(angles) + np.sin(angles)) / np.sqrt(length)


def coulomb(length):
    positions = np.arange(length)
    frequency = np.where(positions <= length // 2, positions, positions - length).astype(float)
    squares = frequency * frequency
    norm_squared = squares[:, None, None] + squares[None, :, None] + squares[None, None, :]
    values = 1.0 / (0.0625 + 25.0 * norm_squared / (length * length))
    values = np.where(norm_squared > 0.5, values, 0.0)
    return values.reshape(length, length * length)


def pieces(total, step=256):
    return [(at, min(step, total - at)) for at in range(0, total, step)]


COMPUTE = True
limit = 16 * 2**20
COMM = True
BACK = True
PRIOR = True
MATE = True
chunk_in = 512
chunk_out = 512


def chunks(total, step):
    starts = list(range(0, max(total - step // 2, 1), step))
    return [slice(at, end) for at, end in zip(starts, starts[1:] + [total])]


def kernel(
    blks,
    orb_hbm, resp_hbm, mask_hbm, zt_hbm, yt_hbm, left_hbm, coul_hbm,
    out_ref,
    orb, resp, mask_ref, zt_ref, yt_ref, left_ref, coul_ref,
    planes, mid, sums, mate, prior, handed, later, total,
    own_sem, table_sem, send_sem, recv_sem,
):
    grp, blk, cross = lax.axis_index("grp"), lax.axis_index("blk"), lax.axis_index("cross")
    length, area = orb.shape
    to_mate = (grp, blk, 1 - cross)
    to_next = (grp, lax.rem(blk + 1, blks), cross)
    to_prev = (grp, lax.rem(blk + blks - 1, blks), cross)

    barrier = pltpu.get_barrier_semaphore()
    for device in (to_mate, to_prev):
        pl.semaphore_signal(barrier, inc=1, device_id=device, device_id_type=MESH)

    own = [
        pltpu.make_async_copy(orb_hbm.at[0], orb, own_sem.at[0]),
        pltpu.make_async_copy(resp_hbm.at[0], resp, own_sem.at[1]),
        pltpu.make_async_copy(mask_hbm, mask_ref, own_sem.at[2]),
    ]
    tables = [
        pltpu.make_async_copy(src, dst, table_sem.at[k])
        for k, (src, dst) in enumerate(
            [(zt_hbm, zt_ref), (yt_hbm, yt_ref), (left_hbm, left_ref), (coul_hbm, coul_ref)]
        )
    ]
    for copy in tables + own:
        copy.start()

    slots = iter(range(64))

    def remote(src, dst, device):
        slot = next(slots)
        return pltpu.make_async_remote_copy(
            src_ref=src, dst_ref=dst, send_sem=send_sem.at[slot], recv_sem=recv_sem.at[slot],
            device_id=device, device_id_type=MESH,
        )

    pl.semaphore_wait(barrier, 2)
    incoming = [
        (
            remote(orb_hbm.at[0, :, part], prior.at[0, :, part], to_next),
            remote(resp_hbm.at[0, :, part], prior.at[1, :, part], to_next),
        )
        for part in chunks(area, chunk_in)
    ]
    from_mate = (
        remote(orb_hbm.at[0], mate.at[0], to_mate),
        remote(resp_hbm.at[0], mate.at[1], to_mate),
    )
    if COMM:
        if MATE:
            for copy in from_mate:
                copy.start()
        for pair in incoming:
            for copy in pair:
                copy.start()

    for copy in tables:
        copy.wait()

    inner = zt_ref[...]

    def fill(pair, carry):
        at = pl.multiple_of(pair * 2 * length, 2 * length)
        rows = yt_ref[pair]
        both = jnp.concatenate([inner * rows[0:1], inner * rows[1:2]], 0)
        planes[pl.ds(at, 2 * length), :] = both.astype(bf16)
        return carry

    if COMPUTE:
        lax.fori_loop(0, length // 2, fill, 0)

    def densities(far, here):
        a, b = orb[:, here].astype(f32), resp[:, here].astype(f32)
        c, d = far[0], far[1]
        return jnp.concatenate([a * c, b * c + a * d], 0).astype(bf16)

    def middle(rows):
        for first in range(0, rows, 2 * length):
            for at, width in pieces(area):
                part = mid[first:first + 2 * length, at:at + width]
                spectrum = jnp.dot(left_ref[...], part, preferred_element_type=f32)
                scale = coul_ref[:, at:at + width]
                filtered = (spectrum * jnp.concatenate([scale, scale], 0)).astype(bf16)
                back = jnp.dot(left_ref[...], filtered, preferred_element_type=f32)
                mid[first:first + 2 * length, at:at + width] = back.astype(bf16)

    whole = slice(0, area)

    for copy in own:
        copy.wait()
    weight = [mask_ref[0, k].astype(f32) for k in range(4)]
    if COMM and MATE:
        for copy in from_mate:
            copy.wait()
    if COMPUTE:
        rows = 4 * length
        first = densities((orb[...].astype(f32), resp[...].astype(f32)), whole)
        second = densities((mate[0].astype(f32), mate[1].astype(f32)), whole)
        values = jnp.concatenate([first, second], 0)
        for at, width in pieces(area):
            mid[:rows, at:at + width] = jnp.dot(
                values, planes[:, at:at + width], preferred_element_type=f32
            ).astype(bf16)
        middle(rows)
        for at, width in pieces(area):
            here = slice(at, at + width)
            fields = jnp.dot(mid[:rows], planes[:, here], preferred_element_type=f32)
            v0, d0 = fields[:length], fields[length:2 * length]
            v1, d1 = fields[2 * length:3 * length], fields[3 * length:]
            total[:, here] = weight[0] * (
                resp[:, here].astype(f32) * v0 + orb[:, here].astype(f32) * d0
            ) + weight[1] * (mate[1, :, here].astype(f32) * v1 + mate[0, :, here].astype(f32) * d1)

    rows = 2 * length
    parts = chunks(area, chunk_in)
    for index, part in enumerate(parts):
        if COMM:
            for copy in incoming[index]:
                copy.wait()
        if COMPUTE and PRIOR:
            values = densities((prior[0, :, part].astype(f32), prior[1, :, part].astype(f32)), part)
            for at, width in pieces(area):
                here = slice(at, at + width)
                product = jnp.dot(values, planes[part, here], preferred_element_type=f32)
                if index:
                    product += sums[:, here]
                if index < len(parts) - 1:
                    sums[:, here] = product
                else:
                    mid[:rows, here] = product.astype(bf16)
    if COMPUTE and PRIOR:
        middle(rows)
    returning = []
    for part in chunks(area, chunk_out):
        if COMPUTE and PRIOR:
            fields = jnp.dot(mid[:rows], planes[:, part], preferred_element_type=f32)
            v, d = fields[:length], fields[length:]
            handed[:, part] = (
                resp[:, part].astype(f32) * v + orb[:, part].astype(f32) * d
            ).astype(bf16)
        returning.append(remote(handed.at[:, part], later.at[:, part], to_prev))
        if COMM and BACK:
            returning[-1].start()
        if COMPUTE and PRIOR:
            total[:, part] += weight[2] * (
                prior[1, :, part].astype(f32) * v + prior[0, :, part].astype(f32) * d
            )
    for part, copy in zip(chunks(area, chunk_out), returning):
        if COMM and BACK:
            copy.wait()
        out_ref[0, :, part] = total[:, part] + weight[3] * later[:, part].astype(f32)


def shards(blks, orbitals, response, pair_mask):
    length, area = orbitals.shape[1:]
    table = cas_table(length)
    inner = np.tile(table, (1, length)).astype(np.float32)
    outer = np.repeat(table, length, 1).astype(np.float32).reshape(length // 2, 2, area)
    left = jnp.asarray(np.kron(np.eye(2), table), bf16)
    kernel_values = coulomb(length).astype(np.float32)
    pinned = pl.BlockSpec(memory_space=pltpu.HBM)
    copies = 2 * len(chunks(area, chunk_in)) + 2 + len(chunks(area, chunk_out))
    stay = functools.partial(pltpu.with_memory_space_constraint, memory_space=pltpu.HBM)
    total = pl.pallas_call(
        functools.partial(kernel, blks),
        out_shape=jax.ShapeDtypeStruct(orbitals.shape, f32),
        in_specs=[pinned] * 7,
        out_specs=pl.BlockSpec(memory_space=pltpu.VMEM),
        scratch_shapes=[
            pltpu.VMEM((length, area), bf16),
            pltpu.VMEM((length, area), bf16),
            pltpu.SMEM(pair_mask.shape, jnp.int32),
            pltpu.VMEM(inner.shape, f32),
            pltpu.VMEM(outer.shape, f32),
            pltpu.VMEM(left.shape, bf16),
            pltpu.VMEM(kernel_values.shape, f32),
            pltpu.VMEM((area, area), bf16),
            pltpu.VMEM((4 * length, area), bf16),
            pltpu.VMEM((2 * length, area), f32),
            pltpu.VMEM((2, length, area), bf16),
            pltpu.VMEM((2, length, area), bf16),
            pltpu.VMEM((length, area), bf16),
            pltpu.VMEM((length, area), bf16),
            pltpu.VMEM((length, area), f32),
            pltpu.SemaphoreType.DMA((3,)),
            pltpu.SemaphoreType.DMA((4,)),
            pltpu.SemaphoreType.DMA((copies,)),
            pltpu.SemaphoreType.DMA((copies,)),
        ],
        compiler_params=pltpu.CompilerParams(collective_id=0, has_side_effects=True, vmem_limit_bytes=limit),
    )(
        stay(orbitals), stay(response), stay(pair_mask),
        *[stay(jnp.asarray(table)) for table in (inner, outer, left, kernel_values)],
    )
    return (-mixing * total).astype(orbitals.dtype)


def solution(mesh):
    spec = P(("grp", "blk", "cross"), None, None)
    return jax.shard_map(
        functools.partial(shards, mesh.shape["blk"]),
        mesh=mesh,
        in_specs=(spec, spec, P(("grp", "blk", "cross"), None)),
        out_specs=spec,
        check_vma=False,
    )
```

```python
import functools

import jax
import jax.numpy as jnp
import numpy as np
from jax import lax
from jax.experimental import pallas as pl
from jax.experimental.pallas import tpu as pltpu
from jax.sharding import PartitionSpec as P

mixing = 0.25
MESH = pl.DeviceIdType.MESH
f32, bf16 = jnp.float32, jnp.bfloat16


def cas_table(length):
    positions = np.arange(length)
    angles = (positions[:, None] * positions[None, :] % length) * (2.0 * np.pi / length)
    return (np.cos(angles) + np.sin(angles)) / np.sqrt(length)


def coulomb(length):
    positions = np.arange(length)
    frequency = np.where(positions <= length // 2, positions, positions - length).astype(float)
    squares = frequency * frequency
    norm_squared = squares[:, None, None] + squares[None, :, None] + squares[None, None, :]
    values = 1.0 / (0.0625 + 25.0 * norm_squared / (length * length))
    values = np.where(norm_squared > 0.5, values, 0.0)
    return values.reshape(length, length * length)


def pieces(total, step=256):
    return [(at, min(step, total - at)) for at in range(0, total, step)]


COMPUTE = True
limit = 16 * 2**20
COMM = True
BACK = True
PRIOR = True
MATE = True
chunk_in = 256
chunk_out = 512


def chunks(total, step):
    starts = list(range(0, max(total - step // 2, 1), step))
    return [slice(at, end) for at, end in zip(starts, starts[1:] + [total])]


def kernel(
    blks,
    orb_hbm, resp_hbm, mask_hbm, zt_hbm, yt_hbm, left_hbm, coul_hbm,
    out_ref,
    orb, resp, mask_ref, zt_ref, yt_ref, left_ref, coul_ref,
    planes, mid, sums, mate, prior, handed, later, total,
    own_sem, table_sem, send_sem, recv_sem,
):
    grp, blk, cross = lax.axis_index("grp"), lax.axis_index("blk"), lax.axis_index("cross")
    length, area = orb.shape
    to_mate = (grp, blk, 1 - cross)
    to_next = (grp, lax.rem(blk + 1, blks), cross)
    to_prev = (grp, lax.rem(blk + blks - 1, blks), cross)

    barrier = pltpu.get_barrier_semaphore()
    for device in (to_mate, to_prev):
        pl.semaphore_signal(barrier, inc=1, device_id=device, device_id_type=MESH)

    own = [
        pltpu.make_async_copy(orb_hbm.at[0], orb, own_sem.at[0]),
        pltpu.make_async_copy(resp_hbm.at[0], resp, own_sem.at[1]),
        pltpu.make_async_copy(mask_hbm, mask_ref, own_sem.at[2]),
    ]
    tables = [
        pltpu.make_async_copy(src, dst, table_sem.at[k])
        for k, (src, dst) in enumerate(
            [(zt_hbm, zt_ref), (yt_hbm, yt_ref), (left_hbm, left_ref), (coul_hbm, coul_ref)]
        )
    ]
    for copy in tables + own:
        copy.start()

    slots = iter(range(64))

    def remote(src, dst, device):
        slot = next(slots)
        return pltpu.make_async_remote_copy(
            src_ref=src, dst_ref=dst, send_sem=send_sem.at[slot], recv_sem=recv_sem.at[slot],
            device_id=device, device_id_type=MESH,
        )

    pl.semaphore_wait(barrier, 2)
    incoming = [
        (
            remote(orb_hbm.at[0, :, part], prior.at[0, :, part], to_next),
            remote(resp_hbm.at[0, :, part], prior.at[1, :, part], to_next),
        )
        for part in chunks(area, chunk_in)
    ]
    from_mate = (
        remote(orb_hbm.at[0], mate.at[0], to_mate),
        remote(resp_hbm.at[0], mate.at[1], to_mate),
    )
    if COMM:
        if MATE:
            for copy in from_mate:
                copy.start()
        for pair in incoming:
            for copy in pair:
                copy.start()

    for copy in tables:
        copy.wait()

    inner = zt_ref[...]

    def fill(pair, carry):
        at = pl.multiple_of(pair * 2 * length, 2 * length)
        rows = yt_ref[pair]
        both = jnp.concatenate([inner * rows[0:1], inner * rows[1:2]], 0)
        planes[pl.ds(at, 2 * length), :] = both.astype(bf16)
        return carry

    if COMPUTE:
        lax.fori_loop(0, length // 2, fill, 0)

    def densities(far, here):
        a, b = orb[:, here].astype(f32), resp[:, here].astype(f32)
        c, d = far[0], far[1]
        return jnp.concatenate([a * c, b * c + a * d], 0).astype(bf16)

    def middle(rows):
        for first in range(0, rows, 2 * length):
            for at, width in pieces(area):
                part = mid[first:first + 2 * length, at:at + width]
                spectrum = jnp.dot(left_ref[...], part, preferred_element_type=f32)
                scale = coul_ref[:, at:at + width]
                filtered = (spectrum * jnp.concatenate([scale, scale], 0)).astype(bf16)
                back = jnp.dot(left_ref[...], filtered, preferred_element_type=f32)
                mid[first:first + 2 * length, at:at + width] = back.astype(bf16)

    whole = slice(0, area)

    for copy in own:
        copy.wait()
    weight = [mask_ref[0, k].astype(f32) for k in range(4)]
    if COMM and MATE:
        for copy in from_mate:
            copy.wait()
    if COMPUTE:
        rows = 4 * length
        first = densities((orb[...].astype(f32), resp[...].astype(f32)), whole)
        second = densities((mate[0].astype(f32), mate[1].astype(f32)), whole)
        values = jnp.concatenate([first, second], 0)
        for at, width in pieces(area):
            mid[:rows, at:at + width] = jnp.dot(
                values, planes[:, at:at + width], preferred_element_type=f32
            ).astype(bf16)
        middle(rows)
        for at, width in pieces(area):
            here = slice(at, at + width)
            fields = jnp.dot(mid[:rows], planes[:, here], preferred_element_type=f32)
            v0, d0 = fields[:length], fields[length:2 * length]
            v1, d1 = fields[2 * length:3 * length], fields[3 * length:]
            total[:, here] = weight[0] * (
                resp[:, here].astype(f32) * v0 + orb[:, here].astype(f32) * d0
            ) + weight[1] * (mate[1, :, here].astype(f32) * v1 + mate[0, :, here].astype(f32) * d1)

    rows = 2 * length
    parts = chunks(area, chunk_in)
    for index, part in enumerate(parts):
        if COMM:
            for copy in incoming[index]:
                copy.wait()
        if COMPUTE and PRIOR:
            values = densities((prior[0, :, part].astype(f32), prior[1, :, part].astype(f32)), part)
            for at, width in pieces(area):
                here = slice(at, at + width)
                product = jnp.dot(values, planes[part, here], preferred_element_type=f32)
                if index:
                    product += sums[:, here]
                if index < len(parts) - 1:
                    sums[:, here] = product
                else:
                    mid[:rows, here] = product.astype(bf16)
    if COMPUTE and PRIOR:
        middle(rows)
    returning = []
    for part in chunks(area, chunk_out):
        if COMPUTE and PRIOR:
            fields = jnp.dot(mid[:rows], planes[:, part], preferred_element_type=f32)
            v, d = fields[:length], fields[length:]
            handed[:, part] = (
                resp[:, part].astype(f32) * v + orb[:, part].astype(f32) * d
            ).astype(bf16)
        returning.append(remote(handed.at[:, part], later.at[:, part], to_prev))
        if COMM and BACK:
            returning[-1].start()
        if COMPUTE and PRIOR:
            total[:, part] += weight[2] * (
                prior[1, :, part].astype(f32) * v + prior[0, :, part].astype(f32) * d
            )
    for part, copy in zip(chunks(area, chunk_out), returning):
        if COMM and BACK:
            copy.wait()
        out_ref[0, :, part] = total[:, part] + weight[3] * later[:, part].astype(f32)


def shards(blks, orbitals, response, pair_mask):
    length, area = orbitals.shape[1:]
    table = cas_table(length)
    inner = np.tile(table, (1, length)).astype(np.float32)
    outer = np.repeat(table, length, 1).astype(np.float32).reshape(length // 2, 2, area)
    left = jnp.asarray(np.kron(np.eye(2), table), bf16)
    kernel_values = coulomb(length).astype(np.float32)
    pinned = pl.BlockSpec(memory_space=pltpu.HBM)
    copies = 2 * len(chunks(area, chunk_in)) + 2 + len(chunks(area, chunk_out))
    stay = functools.partial(pltpu.with_memory_space_constraint, memory_space=pltpu.HBM)
    total = pl.pallas_call(
        functools.partial(kernel, blks),
        out_shape=jax.ShapeDtypeStruct(orbitals.shape, f32),
        in_specs=[pinned] * 7,
        out_specs=pl.BlockSpec(memory_space=pltpu.VMEM),
        scratch_shapes=[
            pltpu.VMEM((length, area), bf16),
            pltpu.VMEM((length, area), bf16),
            pltpu.SMEM(pair_mask.shape, jnp.int32),
            pltpu.VMEM(inner.shape, f32),
            pltpu.VMEM(outer.shape, f32),
            pltpu.VMEM(left.shape, bf16),
            pltpu.VMEM(kernel_values.shape, f32),
            pltpu.VMEM((area, area), bf16),
            pltpu.VMEM((4 * length, area), bf16),
            pltpu.VMEM((2 * length, area), f32),
            pltpu.VMEM((2, length, area), bf16),
            pltpu.VMEM((2, length, area), bf16),
            pltpu.VMEM((length, area), bf16),
            pltpu.VMEM((length, area), bf16),
            pltpu.VMEM((length, area), f32),
            pltpu.SemaphoreType.DMA((3,)),
            pltpu.SemaphoreType.DMA((4,)),
            pltpu.SemaphoreType.DMA((copies,)),
            pltpu.SemaphoreType.DMA((copies,)),
        ],
        compiler_params=pltpu.CompilerParams(collective_id=0, has_side_effects=True, vmem_limit_bytes=limit),
    )(
        stay(orbitals), stay(response), stay(pair_mask),
        *[stay(jnp.asarray(table)) for table in (inner, outer, left, kernel_values)],
    )
    return (-mixing * total).astype(orbitals.dtype)


def solution(mesh):
    spec = P(("grp", "blk", "cross"), None, None)
    return jax.shard_map(
        functools.partial(shards, mesh.shape["blk"]),
        mesh=mesh,
        in_specs=(spec, spec, P(("grp", "blk", "cross"), None)),
        out_specs=spec,
        check_vma=False,
    )
```

```python
import functools

import jax
import jax.numpy as jnp
import numpy as np
from jax import lax
from jax.experimental import pallas as pl
from jax.experimental.pallas import tpu as pltpu
from jax.sharding import PartitionSpec as P

mixing = 0.25
MESH = pl.DeviceIdType.MESH
f32, bf16 = jnp.float32, jnp.bfloat16


def cas_table(length):
    positions = np.arange(length)
    angles = (positions[:, None] * positions[None, :] % length) * (2.0 * np.pi / length)
    return (np.cos(angles) + np.sin(angles)) / np.sqrt(length)


def coulomb(length):
    positions = np.arange(length)
    frequency = np.where(positions <= length // 2, positions, positions - length).astype(float)
    squares = frequency * frequency
    norm_squared = squares[:, None, None] + squares[None, :, None] + squares[None, None, :]
    values = 1.0 / (0.0625 + 25.0 * norm_squared / (length * length))
    values = np.where(norm_squared > 0.5, values, 0.0)
    return values.reshape(length, length * length)


def pieces(total, step=256):
    return [(at, min(step, total - at)) for at in range(0, total, step)]


COMPUTE = True
limit = 16 * 2**20
COMM = True
BACK = True
PRIOR = True
MATE = True
chunk_in = 256
chunk_out = 512


def chunks(total, step):
    starts = list(range(0, max(total - step // 2, 1), step))
    return [slice(at, end) for at, end in zip(starts, starts[1:] + [total])]


def kernel(
    blks,
    orb_hbm, resp_hbm, mask_hbm, zt_hbm, yt_hbm, left_hbm, coul_hbm,
    out_ref,
    orb, resp, mask_ref, zt_ref, yt_ref, left_ref, coul_ref,
    planes, mid, sums, mate, prior, handed, later, total,
    own_sem, table_sem, send_sem, recv_sem,
):
    grp, blk, cross = lax.axis_index("grp"), lax.axis_index("blk"), lax.axis_index("cross")
    length, area = orb.shape
    to_mate = (grp, blk, 1 - cross)
    to_next = (grp, lax.rem(blk + 1, blks), cross)
    to_prev = (grp, lax.rem(blk + blks - 1, blks), cross)

    barrier = pltpu.get_barrier_semaphore()
    for device in (to_prev, to_mate):
        pl.semaphore_signal(barrier, inc=1, device_id=device, device_id_type=MESH)

    own = [
        pltpu.make_async_copy(orb_hbm.at[0], orb, own_sem.at[0]),
        pltpu.make_async_copy(resp_hbm.at[0], resp, own_sem.at[1]),
        pltpu.make_async_copy(mask_hbm, mask_ref, own_sem.at[2]),
    ]
    tables = [
        pltpu.make_async_copy(src, dst, table_sem.at[k])
        for k, (src, dst) in enumerate(
            [(zt_hbm, zt_ref), (yt_hbm, yt_ref), (left_hbm, left_ref), (coul_hbm, coul_ref)]
        )
    ]
    for copy in tables + own:
        copy.start()

    slots = iter(range(64))

    def remote(src, dst, device):
        slot = next(slots)
        return pltpu.make_async_remote_copy(
            src_ref=src, dst_ref=dst, send_sem=send_sem.at[slot], recv_sem=recv_sem.at[slot],
            device_id=device, device_id_type=MESH,
        )

    pl.semaphore_wait(barrier, 2)
    incoming = [
        (
            remote(orb_hbm.at[0, :, part], prior.at[0, :, part], to_next),
            remote(resp_hbm.at[0, :, part], prior.at[1, :, part], to_next),
        )
        for part in chunks(area, chunk_in)
    ]
    from_mate = (
        remote(orb_hbm.at[0], mate.at[0], to_mate),
        remote(resp_hbm.at[0], mate.at[1], to_mate),
    )
    if COMM:
        if MATE:
            for copy in from_mate:
                copy.start()
        for pair in incoming:
            for copy in pair:
                copy.start()

    for copy in tables:
        copy.wait()

    inner = zt_ref[...]

    def fill(pair, carry):
        at = pl.multiple_of(pair * 2 * length, 2 * length)
        rows = yt_ref[pair]
        both = jnp.concatenate([inner * rows[0:1], inner * rows[1:2]], 0)
        planes[pl.ds(at, 2 * length), :] = both.astype(bf16)
        return carry

    if COMPUTE:
        lax.fori_loop(0, length // 2, fill, 0)

    def densities(far, here):
        a, b = orb[:, here].astype(f32), resp[:, here].astype(f32)
        c, d = far[0], far[1]
        return jnp.concatenate([a * c, b * c + a * d], 0).astype(bf16)

    def middle(rows):
        for first in range(0, rows, 2 * length):
            for at, width in pieces(area):
                part = mid[first:first + 2 * length, at:at + width]
                spectrum = jnp.dot(left_ref[...], part, preferred_element_type=f32)
                scale = coul_ref[:, at:at + width]
                filtered = (spectrum * jnp.concatenate([scale, scale], 0)).astype(bf16)
                back = jnp.dot(left_ref[...], filtered, preferred_element_type=f32)
                mid[first:first + 2 * length, at:at + width] = back.astype(bf16)

    whole = slice(0, area)

    for copy in own:
        copy.wait()
    weight = [mask_ref[0, k].astype(f32) for k in range(4)]
    if COMM and MATE:
        for copy in from_mate:
            copy.wait()
    if COMPUTE:
        rows = 4 * length
        first = densities((orb[...].astype(f32), resp[...].astype(f32)), whole)
        second = densities((mate[0].astype(f32), mate[1].astype(f32)), whole)
        values = jnp.concatenate([first, second], 0)
        for at, width in pieces(area):
            mid[:rows, at:at + width] = jnp.dot(
                values, planes[:, at:at + width], preferred_element_type=f32
            ).astype(bf16)
        middle(rows)
        for at, width in pieces(area):
            here = slice(at, at + width)
            fields = jnp.dot(mid[:rows], planes[:, here], preferred_element_type=f32)
            v0, d0 = fields[:length], fields[length:2 * length]
            v1, d1 = fields[2 * length:3 * length], fields[3 * length:]
            total[:, here] = weight[0] * (
                resp[:, here].astype(f32) * v0 + orb[:, here].astype(f32) * d0
            ) + weight[1] * (mate[1, :, here].astype(f32) * v1 + mate[0, :, here].astype(f32) * d1)

    rows = 2 * length
    parts = chunks(area, chunk_in)
    for index, part in enumerate(parts):
        if COMM:
            for copy in incoming[index]:
                copy.wait()
        if COMPUTE and PRIOR:
            values = densities((prior[0, :, part].astype(f32), prior[1, :, part].astype(f32)), part)
            for at, width in pieces(area):
                here = slice(at, at + width)
                product = jnp.dot(values, planes[part, here], preferred_element_type=f32)
                if index:
                    product += sums[:, here]
                if index < len(parts) - 1:
                    sums[:, here] = product
                else:
                    mid[:rows, here] = product.astype(bf16)
    if COMPUTE and PRIOR:
        middle(rows)
    returning = []
    for part in chunks(area, chunk_out):
        if COMPUTE and PRIOR:
            fields = jnp.dot(mid[:rows], planes[:, part], preferred_element_type=f32)
            v, d = fields[:length], fields[length:]
            handed[:, part] = (
                resp[:, part].astype(f32) * v + orb[:, part].astype(f32) * d
            ).astype(bf16)
        returning.append(remote(handed.at[:, part], later.at[:, part], to_prev))
        if COMM and BACK:
            returning[-1].start()
        if COMPUTE and PRIOR:
            total[:, part] += weight[2] * (
                prior[1, :, part].astype(f32) * v + prior[0, :, part].astype(f32) * d
            )
    for part, copy in zip(chunks(area, chunk_out), returning):
        if COMM and BACK:
            copy.wait()
        out_ref[0, :, part] = total[:, part] + weight[3] * later[:, part].astype(f32)


def shards(blks, orbitals, response, pair_mask):
    length, area = orbitals.shape[1:]
    table = cas_table(length)
    inner = np.tile(table, (1, length)).astype(np.float32)
    outer = np.repeat(table, length, 1).astype(np.float32).reshape(length // 2, 2, area)
    left = jnp.asarray(np.kron(np.eye(2), table), bf16)
    kernel_values = coulomb(length).astype(np.float32)
    pinned = pl.BlockSpec(memory_space=pltpu.HBM)
    copies = 2 * len(chunks(area, chunk_in)) + 2 + len(chunks(area, chunk_out))
    stay = functools.partial(pltpu.with_memory_space_constraint, memory_space=pltpu.HBM)
    total = pl.pallas_call(
        functools.partial(kernel, blks),
        out_shape=jax.ShapeDtypeStruct(orbitals.shape, f32),
        in_specs=[pinned] * 7,
        out_specs=pl.BlockSpec(memory_space=pltpu.VMEM),
        scratch_shapes=[
            pltpu.VMEM((length, area), bf16),
            pltpu.VMEM((length, area), bf16),
            pltpu.SMEM(pair_mask.shape, jnp.int32),
            pltpu.VMEM(inner.shape, f32),
            pltpu.VMEM(outer.shape, f32),
            pltpu.VMEM(left.shape, bf16),
            pltpu.VMEM(kernel_values.shape, f32),
            pltpu.VMEM((area, area), bf16),
            pltpu.VMEM((4 * length, area), bf16),
            pltpu.VMEM((2 * length, area), f32),
            pltpu.VMEM((2, length, area), bf16),
            pltpu.VMEM((2, length, area), bf16),
            pltpu.VMEM((length, area), bf16),
            pltpu.VMEM((length, area), bf16),
            pltpu.VMEM((length, area), f32),
            pltpu.SemaphoreType.DMA((3,)),
            pltpu.SemaphoreType.DMA((4,)),
            pltpu.SemaphoreType.DMA((copies,)),
            pltpu.SemaphoreType.DMA((copies,)),
        ],
        compiler_params=pltpu.CompilerParams(collective_id=0, has_side_effects=True, vmem_limit_bytes=limit),
    )(
        stay(orbitals), stay(response), stay(pair_mask),
        *[stay(jnp.asarray(table)) for table in (inner, outer, left, kernel_values)],
    )
    return (-mixing * total).astype(orbitals.dtype)


def solution(mesh):
    spec = P(("grp", "blk", "cross"), None, None)
    return jax.shard_map(
        functools.partial(shards, mesh.shape["blk"]),
        mesh=mesh,
        in_specs=(spec, spec, P(("grp", "blk", "cross"), None)),
        out_specs=spec,
        check_vma=False,
    )
```
